32 devices in a mesh: sec: 4 (over y, x), col: 8 (over z, core).
Axes of the slice: x: 2, y: 2, z: 4, core: 2. Of those that a mesh axis runs over, the one named last changes fastest.
Arguments:
- matrix_rows: float32 [4096, 16384], P('sec', 'col'), may hold values from -6 to 6
- factor_bank: float32 [4, 8, 512, 512], P(None, 'sec', 'col'), may hold values from -1 to 1, as said below
- owner_table: int32 [4, 8, 8], P(None, 'sec'), may hold values from 0 to 7, each once within a row
Outputs:
- updated: float32 [4096, 16384], P('sec', 'col')
The draws below stay inside these ranges and needn't reach their ends.
Inputs may be any that keep to these rules, and one draw needn't show every extreme that they name: `factor_bank`: each factor G[r,k] is orthogonal. `owner_table`: for each round and section the list names every row block once.
All inputs are finite; a program needn't handle non-finite values.
Results may differ from the reference program's by a relative error of at most 0.00014.
Values sent between devices are 32-bit elements; how exact they have to be, the bound alone decides.
A program may use at most 128 MiB of HBM per device.

```python
import jax
import jax.numpy as jnp
from jax import lax

F = 512
ROUNDS = 4
SECTIONS = 8
ROWS = 4096
CUT = 16384
N_COL = 8


def draw_factor_bank(key, part):
    raw = jax.random.normal(key, (ROUNDS, SECTIONS, F, F), jnp.float32)
    orthogonal, upper = jnp.linalg.qr(raw)
    return orthogonal


def level_of(stream_key, shape, split, low, largest):
    loudness, own = 1.0, jax.random.fold_in(stream_key, 6)
    for dim, shards_of in split:
        draws = jnp.exp(jax.random.uniform(jax.random.fold_in(own, dim), (shards_of,), jnp.float32, low / len(split), largest / len(split)))
        loudness = loudness * jnp.repeat(draws, shape[dim] // shards_of).reshape([-1 if axis == dim else 1 for axis in range(len(shape))])
    return loudness


def centred(stream_key, dims, deviation, most, pieces=(), held_as=jnp.bfloat16):
    array = jax.random.normal(stream_key, dims, jnp.float32) * deviation
    if len(pieces) > 0:
        array = level_of(stream_key, dims, pieces, -0.22, 0.18) * array
    return jnp.clip(array, min=-most, max=most).astype(held_as)


def setup_inputs(seed: int = 0) -> dict:
    seeds = jax.random.split(jax.random.key(seed), 4)
    matrix_rows = centred(seeds[0], (ROWS, CUT), 1.0, 6.0, ((0, 4), (1, 8)), jnp.float32)
    factor_bank = draw_factor_bank(jax.random.fold_in(seeds[3], 71), 0)
    owner_table = jax.vmap(lambda own: jax.random.permutation(own, N_COL))(jax.random.split(seeds[2], ROUNDS * SECTIONS)).reshape((ROUNDS, SECTIONS, N_COL)).astype(jnp.int32)
    return {"matrix_rows": matrix_rows, "factor_bank": factor_bank, "owner_table": owner_table}


def assemble(stored, owner_now):
    sections = stored.shape[0]
    extent = stored.shape[1]
    groups = owner_now.shape[1]
    blocks = stored.reshape(sections, groups, extent // groups, extent)
    labels = jnp.arange(groups, dtype=jnp.int32)
    onehot = (owner_now[:, :, None] == labels[None, None, :]).astype(stored.dtype)
    placed = jnp.einsum('scb,scnf->sbnf', onehot, blocks, precision=lax.Precision.HIGHEST)
    return placed.reshape(sections, extent, extent)

def reference(matrix_rows, factor_bank, owner_table):
    current = matrix_rows
    for number in range(ROUNDS):
        factors = assemble(factor_bank[number], owner_table[number])
        if number % 2 == 1:
            current = jnp.roll(current, F // 2, axis=0)
        windows = current.reshape(SECTIONS, F, -1)
        current = lax.map(lambda couple: jnp.dot(couple[0], couple[1], precision=lax.Precision.HIGHEST), (factors, windows))
        current = current.reshape(SECTIONS * F, -1)
        if number % 2 == 1:
            current = jnp.roll(current, -(F // 2), axis=0)
    return current
```

```python
import jax
import jax.numpy as jnp
from jax import lax
from jax.sharding import PartitionSpec as P

ROUNDS = 4
CHUNKS = 4


def shifted_2(value, axis, steps):
    count = lax.axis_size(axis)
    pairs = [(source, (source + steps) % count) for source in range(count)]
    return lax.ppermute(value, axis, pairs)


def assemble(gathered, owner_now):
    sections = gathered.shape[0]
    extent = gathered.shape[1]
    groups = owner_now.shape[1]
    blocks = gathered.reshape(sections, groups, extent // groups, extent)
    labels = jnp.arange(groups, dtype=jnp.int32)
    onehot = (owner_now[:, :, None] == labels[None, None, :]).astype(gathered.dtype)
    placed = jnp.einsum("scb,scnf->sbnf", onehot, blocks, precision=lax.Precision.HIGHEST)
    return placed.reshape(sections, extent, extent)


def rotate(factor, window):
    return jnp.dot(factor, window, precision=lax.Precision.HIGH)


def local(matrix_rows, factor_bank, owner_table):
    sections = owner_table.shape[1]
    extent = factor_bank.shape[3]
    halfway = extent // 2
    columns = matrix_rows.shape[1]
    chunks = CHUNKS if columns % (CHUNKS * 128) == 0 else 1
    width = columns // chunks
    state = [
        [
            matrix_rows[k * extent : (k + 1) * extent, c * width : (c + 1) * width]
            for k in range(sections)
        ]
        for c in range(chunks)
    ]
    for number in range(ROUNDS):
        row_blocks = lax.all_gather(factor_bank[number], "col", axis=1, tiled=True)
        factors = assemble(row_blocks, owner_table[number])
        for c in range(chunks):
            now = state[c]
            if number % 2 == 0:
                order = list(range(sections - 1, -1, -1))
                done = {k: rotate(factors[k], now[k]) for k in order}
                state[c] = [done[k] for k in range(sections)]
            else:
                arrived = shifted_2(now[-1][halfway:], "sec", 1)
                interior = [
                    rotate(
                        factors[k],
                        jnp.concatenate([now[k - 1][halfway:], now[k][:halfway]], axis=0),
                    )
                    for k in range(1, sections)
                ]
                border = rotate(
                    factors[0], jnp.concatenate([arrived, now[0][:halfway]], axis=0)
                )
                returned = shifted_2(border[:halfway], "sec", -1)
                shifted = [border] + interior
                state[c] = [
                    jnp.concatenate(
                        [
                            shifted[k][halfway:],
                            shifted[k + 1][:halfway] if k + 1 < sections else returned,
                        ],
                        axis=0,
                    )
                    for k in range(sections)
                ]
    return jnp.concatenate([jnp.concatenate(now, axis=0) for now in state], axis=1)


def solution(mesh):
    in_specs = (P("sec", "col"), P(None, "sec", "col", None), P(None, "sec", None))
    out_specs = P("sec", "col")
    return jax.shard_map(local, mesh=mesh, in_specs=in_specs, out_specs=out_specs, check_vma=False)
```

```python
import functools

import jax
import jax.numpy as jnp
from jax import lax
from jax.experimental import pallas as pl
from jax.experimental.pallas import tpu as pltpu
from jax.sharding import PartitionSpec as P

ROUNDS = 4
CHUNKS = 4


def shifted_2(value, axis, steps):
    count = lax.axis_size(axis)
    pairs = [(source, (source + steps) % count) for source in range(count)]
    return lax.ppermute(value, axis, pairs)


def gather_kernel(count, table_ref, own_ref, after_ref, out_ref, held, local_sem, up_sems, down_sems, pair_sems):
    chips = count // 2
    ups, downs = chips // 2, (chips - 1) // 2
    me = lax.axis_index("col")
    chip, core = me // 2, me % 2
    up = ((chip + 1) % chips) * 2 + core
    down = ((chip + chips - 1) % chips) * 2 + core
    partner = chip * 2 + 1 - core

    barrier = pltpu.get_barrier_semaphore()
    for other in (up, down, partner):
        pl.semaphore_signal(
            barrier, inc=1, device_id={"col": other}, device_id_type=pl.DeviceIdType.MESH
        )
    pl.semaphore_wait(barrier, 3)

    def send(src, slot, target, sems, at):
        copy = pltpu.make_async_remote_copy(
            src_ref=src,
            dst_ref=held.at[slot],
            send_sem=sems.at[0, at],
            recv_sem=sems.at[1, at],
            device_id={"col": target},
            device_id_type=pl.DeviceIdType.MESH,
        )
        copy.start()
        return copy

    up_copies = [send(own_ref, me, up, up_sems, 0)]
    down_copies = [send(own_ref, me, down, down_sems, 0)] if downs else []
    pair_copies = [send(own_ref, me, partner, pair_sems, 0)]
    mine = pltpu.make_async_copy(own_ref, held.at[me], local_sem)
    mine.start()
    for step in range(1, ups + 1):
        slot = ((chip + chips - step) % chips) * 2 + core
        up_copies[step - 1].wait_recv()
        if step < ups:
            up_copies.append(send(held.at[slot], slot, up, up_sems, step))
        pair_copies.append(send(held.at[slot], slot, partner, pair_sems, len(pair_copies)))
        if step <= downs:
            slot = ((chip + step) % chips) * 2 + core
            down_copies[step - 1].wait_recv()
            if step < downs:
                down_copies.append(send(held.at[slot], slot, down, down_sems, step))
            pair_copies.append(send(held.at[slot], slot, partner, pair_sems, len(pair_copies)))
    for copy in pair_copies:
        copy.wait_recv()
    for copy in up_copies + down_copies + pair_copies:
        copy.wait_send()
    mine.wait()

    sections, rows = own_ref.shape[0], own_ref.shape[1]
    for k in range(sections):
        for b in range(count):
            place = jnp.int32(0)
            for c in range(count):
                place = jnp.where(table_ref[k, c] == b, c, place)
            out_ref[k, b * rows : (b + 1) * rows, :] = held[place, k]


def gather(own, table, after, ident):
    count = lax.axis_size("col")
    sections, rows, extent = own.shape
    chips = count // 2
    return pl.pallas_call(
        functools.partial(gather_kernel, count),
        out_shape=jax.ShapeDtypeStruct((sections, extent, extent), own.dtype),
        in_specs=[
            pl.BlockSpec(memory_space=pltpu.SMEM),
            pl.BlockSpec(memory_space=pltpu.VMEM),
            pl.BlockSpec(memory_space=pltpu.VMEM),
        ],
        out_specs=pl.BlockSpec(memory_space=pltpu.VMEM),
        scratch_shapes=[
            pltpu.VMEM((count, sections, rows, extent), own.dtype),
            pltpu.SemaphoreType.DMA,
            pltpu.SemaphoreType.DMA((2, max(chips // 2, 1))),
            pltpu.SemaphoreType.DMA((2, max((chips - 1) // 2, 1))),
            pltpu.SemaphoreType.DMA((2, chips)),
        ],
        compiler_params=pltpu.CompilerParams(
            collective_id=ident, has_side_effects=True, vmem_limit_bytes=16 << 20
        ),
        cost_estimate=pl.CostEstimate(
            flops=0, bytes_accessed=32 * own.size * own.dtype.itemsize, transcendentals=0
        ),
        name=f"gather_{ident}",
    )(table, own, after)


def rotate(factor, window):
    return jnp.dot(factor, window, precision=lax.Precision.HIGH)


def local(matrix_rows, factor_bank, owner_table):
    sections = owner_table.shape[1]
    extent = factor_bank.shape[3]
    halfway = extent // 2
    columns = matrix_rows.shape[1]
    chunks = CHUNKS if columns % (CHUNKS * 128) == 0 else 1
    width = columns // chunks
    state = [
        [
            matrix_rows[k * extent : (k + 1) * extent, c * width : (c + 1) * width]
            for k in range(sections)
        ]
        for c in range(chunks)
    ]
    after = matrix_rows[:8, :128]
    finished, last = [], []
    for number in range(ROUNDS):
        factors = gather(factor_bank[number], owner_table[number], after, number)
        marks = []
        for c in range(chunks):
            now = state[c]
            if number % 2 == 0:
                done = {k: rotate(factors[k], now[k]) for k in range(sections - 1, -1, -1)}
                state[c] = [done[k] for k in range(sections)]
                marks.append(done[sections - 1][:8, :128])
            else:
                arrived = shifted_2(now[-1][halfway:], "sec", 1)
                interior = [
                    rotate(
                        factors[k],
                        jnp.concatenate([now[k - 1][halfway:], now[k][:halfway]], axis=0),
                    )
                    for k in range(1, sections)
                ]
                border = rotate(
                    factors[0], jnp.concatenate([arrived, now[0][:halfway]], axis=0)
                )
                returned = shifted_2(border[:halfway], "sec", -1)
                marks.append(border[:8, :128])
                shifted = [border] + interior
                if number == ROUNDS - 1:
                    finished.append([border[halfway:]] + interior)
                    last.append(returned)
                    continue
                state[c] = [
                    jnp.concatenate(
                        [
                            shifted[k][halfway:],
                            shifted[k + 1][:halfway] if k + 1 < sections else returned,
                        ],
                        axis=0,
                    )
                    for k in range(sections)
                ]
        if number == 0:
            after = marks[-1]
        elif number == 1:
            after = marks[min(1, chunks - 1)]
            late = marks[-1]
        elif number == 2:
            after = late
    result = jnp.broadcast_to(marks[0][0, 0], matrix_rows.shape)
    for c in range(chunks):
        row = 0
        for piece in finished[c]:
            result = lax.dynamic_update_slice(result, piece, (row, c * width))
            row += piece.shape[0]
    for c in range(chunks):
        result = lax.dynamic_update_slice(
            result, last[c], (matrix_rows.shape[0] - halfway, c * width)
        )
    return result


def solution(mesh):
    in_specs = (P("sec", "col"), P(None, "sec", "col", None), P(None, "sec", None))
    out_specs = P("sec", "col")
    return jax.shard_map(local, mesh=mesh, in_specs=in_specs, out_specs=out_specs, check_vma=False)
```

```python
import functools

import jax
import jax.numpy as jnp
from jax import lax
from jax.experimental import pallas as pl
from jax.experimental.pallas import tpu as pltpu
from jax.sharding import PartitionSpec as P

ROUNDS = 4
CHUNKS = 4


def shifted_2(value, axis, steps):
    count = lax.axis_size(axis)
    pairs = [(source, (source + steps) % count) for source in range(count)]
    return lax.ppermute(value, axis, pairs)


def gather_kernel(count, table_ref, own_ref, after_ref, out_ref, held, local_sem, up_sems, down_sems, pair_sems):
    chips = count // 2
    ups, downs = chips // 2, (chips - 1) // 2
    me = lax.axis_index("col")
    chip, core = me // 2, me % 2
    up = ((chip + 1) % chips) * 2 + core
    down = ((chip + chips - 1) % chips) * 2 + core
    partner = chip * 2 + 1 - core

    barrier = pltpu.get_barrier_semaphore()
    for other in (up, down, partner):
        pl.semaphore_signal(
            barrier, inc=1, device_id={"col": other}, device_id_type=pl.DeviceIdType.MESH
        )
    pl.semaphore_wait(barrier, 3)

    def send(src, slot, target, sems, at):
        copy = pltpu.make_async_remote_copy(
            src_ref=src,
            dst_ref=held.at[slot],
            send_sem=sems.at[0, at],
            recv_sem=sems.at[1, at],
            device_id={"col": target},
            device_id_type=pl.DeviceIdType.MESH,
        )
        copy.start()
        return copy

    up_copies = [send(own_ref, me, up, up_sems, 0)]
    down_copies = [send(own_ref, me, down, down_sems, 0)] if downs else []
    pair_copies = [send(own_ref, me, partner, pair_sems, 0)]
    mine = pltpu.make_async_copy(own_ref, held.at[me], local_sem)
    mine.start()
    for step in range(1, ups + 1):
        slot = ((chip + chips - step) % chips) * 2 + core
        up_copies[step - 1].wait_recv()
        if step < ups:
            up_copies.append(send(held.at[slot], slot, up, up_sems, step))
        pair_copies.append(send(held.at[slot], slot, partner, pair_sems, len(pair_copies)))
        if step <= downs:
            slot = ((chip + step) % chips) * 2 + core
            down_copies[step - 1].wait_recv()
            if step < downs:
                down_copies.append(send(held.at[slot], slot, down, down_sems, step))
            pair_copies.append(send(held.at[slot], slot, partner, pair_sems, len(pair_copies)))
    for copy in pair_copies:
        copy.wait_recv()
    for copy in up_copies + down_copies + pair_copies:
        copy.wait_send()
    mine.wait()

    sections, rows = own_ref.shape[0], own_ref.shape[1]
    for k in range(sections):
        for b in range(count):
            place = jnp.int32(0)
            for c in range(count):
                place = jnp.where(table_ref[k, c] == b, c, place)
            out_ref[k, b * rows : (b + 1) * rows, :] = held[place, k]


def gather(own, table, after, ident):
    count = lax.axis_size("col")
    sections, rows, extent = own.shape
    chips = count // 2
    return pl.pallas_call(
        functools.partial(gather_kernel, count),
        out_shape=jax.ShapeDtypeStruct((sections, extent, extent), own.dtype),
        in_specs=[
            pl.BlockSpec(memory_space=pltpu.SMEM),
            pl.BlockSpec(memory_space=pltpu.VMEM),
            pl.BlockSpec(memory_space=pltpu.VMEM),
        ],
        out_specs=pl.BlockSpec(memory_space=pltpu.VMEM),
        scratch_shapes=[
            pltpu.VMEM((count, sections, rows, extent), own.dtype),
            pltpu.SemaphoreType.DMA,
            pltpu.SemaphoreType.DMA((2, max(chips // 2, 1))),
            pltpu.SemaphoreType.DMA((2, max((chips - 1) // 2, 1))),
            pltpu.SemaphoreType.DMA((2, chips)),
        ],
        compiler_params=pltpu.CompilerParams(
            collective_id=ident, has_side_effects=True, vmem_limit_bytes=16 << 20
        ),
        cost_estimate=pl.CostEstimate(
            flops=0, bytes_accessed=32 * own.size * own.dtype.itemsize, transcendentals=0
        ),
        name=f"gather_{ident}",
    )(table, own, after)


def rotate(factor, window):
    return jnp.dot(factor, window, precision=lax.Precision.HIGH)


def local(matrix_rows, factor_bank, owner_table):
    sections = owner_table.shape[1]
    extent = factor_bank.shape[3]
    halfway = extent // 2
    columns = matrix_rows.shape[1]
    chunks = CHUNKS if columns % (CHUNKS * 128) == 0 else 1
    width = columns // chunks
    state = [
        [
            matrix_rows[k * extent : (k + 1) * extent, c * width : (c + 1) * width]
            for k in range(sections)
        ]
        for c in range(chunks)
    ]
    after = matrix_rows[:8, :128]
    finished, last = [], []
    for number in range(ROUNDS):
        marks = []
        if number == 0 and sections > 1:
            final = gather(factor_bank[0, -1:], owner_table[0, -1:], after, ROUNDS)
            ends = [rotate(final[0], now[-1]) for now in state]
            rest = gather(factor_bank[0, :-1], owner_table[0, :-1], ends[-1][:8, :128], 0)
            for c in range(chunks):
                now = state[c]
                state[c] = [rotate(rest[k], now[k]) for k in range(sections - 1)] + [ends[c]]
            after = state[-1][0][:8, :128]
            continue
        factors = gather(factor_bank[number], owner_table[number], after, number)
        for c in range(chunks):
            now = state[c]
            if number % 2 == 0:
                done = {k: rotate(factors[k], now[k]) for k in range(sections - 1, -1, -1)}
                state[c] = [done[k] for k in range(sections)]
                marks.append(done[sections - 1][:8, :128])
            else:
                arrived = shifted_2(now[-1][halfway:], "sec", 1)
                interior = [
                    rotate(
                        factors[k],
                        jnp.concatenate([now[k - 1][halfway:], now[k][:halfway]], axis=0),
                    )
                    for k in range(1, sections)
                ]
                border = rotate(
                    factors[0], jnp.concatenate([arrived, now[0][:halfway]], axis=0)
                )
                returned = shifted_2(border[:halfway], "sec", -1)
                marks.append(border[:8, :128])
                shifted = [border] + interior
                if number == ROUNDS - 1:
                    finished.append([border[halfway:]] + interior)
                    last.append(returned)
                    continue
                state[c] = [
                    jnp.concatenate(
                        [
                            shifted[k][halfway:],
                            shifted[k + 1][:halfway] if k + 1 < sections else returned,
                        ],
                        axis=0,
                    )
                    for k in range(sections)
                ]
        if number == 0:
            after = marks[-1]
        elif number == 1:
            after = marks[min(1, chunks - 1)]
        elif number == 2:
            after = marks[min(1, chunks - 1)]
    result = jnp.broadcast_to(marks[0][0, 0], matrix_rows.shape)
    for c in range(chunks):
        row = 0
        for piece in finished[c]:
            result = lax.dynamic_update_slice(result, piece, (row, c * width))
            row += piece.shape[0]
    for c in range(chunks):
        result = lax.dynamic_update_slice(
            result, last[c], (matrix_rows.shape[0] - halfway, c * width)
        )
    return result


def solution(mesh):
    in_specs = (P("sec", "col"), P(None, "sec", "col", None), P(None, "sec", None))
    out_specs = P("sec", "col")
    return jax.shard_map(local, mesh=mesh, in_specs=in_specs, out_specs=out_specs, check_vma=False)
```
